32 devices in a mesh: ctx: 16 (over z, y, core), tp: 2 (over x).
Axes of the slice: x: 2, y: 2, z: 4, core: 2. Of those that a mesh axis runs over, the one named last changes fastest.
Arguments:
- xbc: bfloat16 [2, 4096, 8, 1280], P(None, 'ctx', 'tp'), may hold values from -6 to 6
- zgate: bfloat16 [2, 4096, 8, 1024], P(None, 'ctx', 'tp'), may hold values from -6 to 6
- dt_raw: float32 [2, 4096, 128], P(None, 'ctx', 'tp'), may hold values from -1.5 to 30
- a_rate: float32 [128], P('tp'), may hold values from 0.00012207031 to 0.04
- d_skip: float32 [128], P('tp'), may hold values from 0.5 to 2
- conv_weight: bfloat16 [8, 4, 1280], P('tp'), may hold values from -3 to 3
- convolution_bias: float32 [8, 1280], P('tp'), may hold values from -3 to 3
- norm_gain: float32 [8, 1024], P('tp'), may hold values from 0.25 to 1.75
- out_weight: bfloat16 [8, 1024, 4096], P('tp', None, 'ctx'), may hold values from -0.0625 to 0.0625
Outputs:
- layer_out: bfloat16 [2, 4096, 4096], P(None, 'ctx', 'tp')
The draws below stay inside these ranges and needn't reach their ends.
All inputs are finite; a program needn't handle non-finite values.
Results may differ from the reference program's by a relative error of at most 0.0054.
Values may be sent and summed in bfloat16 or wider, within the bound.
No kernel may reach another device: no remote copies, remote signals or barrier semaphores. Data moves between devices by JAX's collectives and lax.ppermute only.
A program may use at most 320 MiB of HBM per device.

```python
import jax
import jax.numpy as jnp
from jax import lax

D = 4096
HEADS = 128
HEAD_DIM = 64
STATE = 128
GROUPS = 8
KW = 4
SPAN = 256
SEQUENCE_COUNT = 2
SEQUENCE_LENGTH = 4096
GX = 1024
GW = 1280


def draw_dt_raw(key, part):
    first_key, second_random_key = jax.random.split(key)
    baseline_sample = jnp.clip(jax.random.normal(first_key, (SEQUENCE_COUNT, SEQUENCE_LENGTH, HEADS), jnp.float32) * 0.6 - 0.25, -1.5, 1.0)
    spike_positions = jax.random.randint(second_random_key, (SEQUENCE_COUNT, 4), 0, SEQUENCE_LENGTH)
    spike_mask = jnp.any(jnp.arange(SEQUENCE_LENGTH)[None, :, None] == spike_positions[:, None, :], axis=-1)
    return jnp.where(spike_mask[:, :, None], 30.0, baseline_sample)


def draw_a_rate(key, part):
    low_log = jnp.log(0.5 / SEQUENCE_LENGTH)
    high_log = jnp.log(0.04)
    log_rate = jax.random.uniform(key, (HEADS,), jnp.float32, low_log, high_log)
    return jnp.exp(log_rate)


def steps_of(own_key, dims, cuts, least, largest):
    level, own = 1.0, jax.random.fold_in(own_key, 6)
    for dim, blocks in cuts:
        draws = jnp.exp(jax.random.uniform(jax.random.fold_in(own, dim), (blocks,), jnp.float32, least / len(cuts), largest / len(cuts)))
        level = level * jnp.repeat(draws, dims[dim] // blocks).reshape([-1 if axis == dim else 1 for axis in range(len(dims))])
    return level


def noise(stream_key, dims, scale, reach, cuts=(), kind=jnp.bfloat16):
    entries = scale * jax.random.normal(stream_key, dims, jnp.float32)
    if cuts:
        entries = entries * steps_of(stream_key, dims, cuts, -0.22, 0.18)
    return jnp.clip(entries, -reach, reach).astype(kind)


def setup_inputs(seed: int = 0) -> dict:
    seeds = jax.random.split(jax.random.key(seed), 10)
    return {
        "xbc": noise(seeds[0], (SEQUENCE_COUNT, SEQUENCE_LENGTH, GROUPS, GW), 1.0, 6.0, ((1, 16), (2, 2))),
        "zgate": noise(seeds[1], (SEQUENCE_COUNT, SEQUENCE_LENGTH, GROUPS, GX), 1.0, 6.0, ((1, 16), (2, 2))),
        "dt_raw": draw_dt_raw(jax.random.fold_in(seeds[9], 71), 0),
        "a_rate": draw_a_rate(jax.random.fold_in(seeds[9], 71), 0),
        "d_skip": jnp.clip(0.5 + 1.5 * jax.random.uniform(seeds[4], (HEADS,), jnp.float32) ** steps_of(seeds[4], (HEADS,), ((0, 2),), -0.2, 0.2), 0.5, 2.0),
        "conv_weight": noise(seeds[5], (GROUPS, KW, GW), KW ** -0.5, 3.0, ((0, 2),)),
        "convolution_bias": noise(seeds[6], (GROUPS, GW), 0.5, 3.0, ((0, 2),), jnp.float32),
        "norm_gain": jnp.clip(1.0 + 0.15 * jax.random.normal(seeds[7], (GROUPS, GX), jnp.float32), 0.25, 1.75),
        "out_weight": noise(seeds[8], (GROUPS, GX, D), (GROUPS * GX) ** -0.5, 0.0625, ((0, 2), (2, 16))),
    }


def ssd_block(carry_state, inputs, a_rate, d_skip):
    x_blk, b_blk, c_blk, dt_blk = inputs
    per_group = HEADS // GROUPS
    log_decay = -a_rate[None, :] * dt_blk
    cum_decay = jnp.cumsum(log_decay, axis=0)
    last_decay = cum_decay[-1]
    gram_blk = jnp.einsum('tgn,rgn->gtr', c_blk.astype(jnp.float32), b_blk.astype(jnp.float32))
    gram_heads = jnp.repeat(gram_blk, per_group, axis=0)
    cum_cols = cum_decay.T
    decay_diff = cum_cols[:, :, None] - cum_cols[:, None, :]
    lower_mask = (jnp.arange(SPAN)[:, None] >= jnp.arange(SPAN)[None, :])[None, :, :]
    decay_mat = jnp.where(lower_mask, jnp.exp(jnp.where(lower_mask, decay_diff, 0.0)), 0.0)
    weights = (gram_heads * decay_mat * dt_blk.T[:, None, :]).astype(jnp.bfloat16)
    y_local = jnp.einsum('htr,rhp->thp', weights.astype(jnp.float32), x_blk.astype(jnp.float32))
    b_heads = jnp.repeat(b_blk, per_group, axis=1)
    scale_b = jnp.exp(last_decay[None, :] - cum_decay) * dt_blk
    weighted_b = (scale_b[:, :, None] * b_heads.astype(jnp.float32)).astype(jnp.bfloat16)
    block_state = jnp.einsum('rhn,rhp->hnp', weighted_b.astype(jnp.float32), x_blk.astype(jnp.float32))
    state_bf = carry_state.astype(jnp.bfloat16)
    c_heads = jnp.repeat(c_blk, per_group, axis=1)
    carried = jnp.einsum('thn,hnp->thp', c_heads.astype(jnp.float32), state_bf.astype(jnp.float32))
    y_carried = jnp.exp(cum_decay)[:, :, None] * carried
    y_total = y_local + y_carried + d_skip[None, :, None] * x_blk.astype(jnp.float32)
    next_state = jnp.exp(last_decay)[:, None, None] * carry_state + block_state
    return (next_state, y_total)

def reference(xbc, zgate, dt_raw, a_rate, d_skip, conv_weight, convolution_bias, norm_gain, out_weight):

    def one_sequence(inputs):
        xbc_seq, zgate_seq, dt_seq = inputs
        padded = jnp.concatenate([jnp.zeros((KW - 1, GROUPS, GW), xbc_seq.dtype), xbc_seq], axis=0)
        pre_act = padded[0:SEQUENCE_LENGTH].astype(jnp.float32) * conv_weight[:, 0, :].astype(jnp.float32)
        for offset in range(1, KW):
            pre_act = pre_act + padded[offset:offset + SEQUENCE_LENGTH].astype(jnp.float32) * conv_weight[:, offset, :].astype(jnp.float32)
        conv_out = jax.nn.silu(pre_act + convolution_bias).astype(jnp.bfloat16)
        block_count = SEQUENCE_LENGTH // SPAN
        x_all = conv_out[:, :, :GX].reshape(block_count, SPAN, HEADS, HEAD_DIM)
        b_all = conv_out[:, :, GX:GX + STATE].reshape(block_count, SPAN, GROUPS, STATE)
        c_all = conv_out[:, :, GX + STATE:].reshape(block_count, SPAN, GROUPS, STATE)
        dt_all = jax.nn.softplus(dt_seq).reshape(block_count, SPAN, HEADS)
        start_state = jnp.zeros((HEADS, STATE, HEAD_DIM), jnp.float32)

        def scan_step(carry_state, block_inputs):
            return ssd_block(carry_state, block_inputs, a_rate, d_skip)
        final_state, y_blocks = lax.scan(scan_step, start_state, (x_all, b_all, c_all, dt_all))
        y_all = y_blocks.reshape(SEQUENCE_LENGTH, GROUPS, GX)
        gated_out = y_all * jax.nn.silu(zgate_seq.astype(jnp.float32))
        mean_sq = lax.optimization_barrier(jnp.mean(gated_out * gated_out, axis=-1, keepdims=True))
        normed = (gated_out * lax.rsqrt(mean_sq + 1e-05) * norm_gain).astype(jnp.bfloat16)
        product = jnp.dot(normed.reshape(SEQUENCE_LENGTH, GROUPS * GX).astype(jnp.float32), out_weight.reshape(GROUPS * GX, D).astype(jnp.float32))
        return product.astype(jnp.bfloat16)
    return lax.map(one_sequence, (xbc, zgate, dt_raw))
```

```python
import functools
import math

import jax
import jax.numpy as jnp
from jax import lax
from jax.experimental import pallas as pl
from jax.experimental.pallas import tpu as pltpu
from jax.sharding import PartitionSpec as P

SPAN = 256
LANES = 128
LOG2E = math.log2(math.e)
F32 = jnp.float32
BF16 = jnp.bfloat16


def sigmoid(v):
    return 0.5 * jnp.tanh(0.5 * v) + 0.5


def lane_pair(col, first, head_size, rows):
    per_tile = LANES // head_size
    lane = lax.broadcasted_iota(jnp.int32, (rows, LANES), 1)
    out = jnp.broadcast_to(col[:, first : first + 1], (rows, LANES))
    for k in range(1, per_tile):
        nxt = jnp.broadcast_to(col[:, first + k : first + k + 1], (rows, LANES))
        out = jnp.where(lane < k * head_size, out, nxt)
    return out


def conv_kernel(x_ref, rim_ref, w_ref, b_ref, scale_ref, conv_ref, state_ref, pad, *, taps, width, head_size):
    rows = x_ref.shape[2]
    chan = x_ref.shape[3]
    base = 8
    pad[base - (taps - 1) : base, :] = rim_ref[0, 0].astype(F32)
    pad[base:, :] = x_ref[0, 0].astype(F32)
    weight = w_ref[0].astype(F32)
    bias = b_ref[0]
    scale = scale_ref[0, 0]

    def chunk(c):
        lanes = slice(c * LANES, (c + 1) * LANES)
        start = base - (taps - 1)
        pre = pad[start : start + rows, lanes] * weight[0:1, lanes]
        for k in range(1, taps):
            pre = pre + pad[start + k : start + k + rows, lanes] * weight[k : k + 1, lanes]
        pre = pre + bias[:, lanes]
        out = (pre * sigmoid(pre)).astype(BF16)
        conv_ref[0, 0, :, lanes] = out
        return out

    tiles = width // LANES
    state_size = (chan - width) // 2
    b_vals = jnp.concatenate([chunk(c) for c in range(tiles, tiles + state_size // LANES)], axis=1)
    for c in range(tiles + state_size // LANES, chan // LANES):
        chunk(c)
    b_turned = b_vals.T
    for c in range(tiles):
        vals = chunk(c)
        spread = lane_pair(scale, c * (LANES // head_size), head_size, rows)
        scaled = (vals.astype(F32) * spread).astype(BF16)
        state_ref[0, c] = jnp.dot(b_turned, scaled, preferred_element_type=F32).astype(BF16)


def inner_kernel(conv_ref, col_ref, row_ref, skip_ref, y_ref, gram_ref, *, width, head_size):
    rows = conv_ref.shape[2]
    chan = conv_ref.shape[3]
    state_size = (chan - width) // 2
    half = rows // 2
    b_vals = conv_ref[0, 0, :, width : width + state_size]
    c_vals = conv_ref[0, 0, :, width + state_size :]
    gram = lax.dot_general(c_vals, b_vals, (((1,), (1,)), ((), ())), preferred_element_type=F32)
    t_pos = lax.broadcasted_iota(jnp.int32, (rows, rows), 0)
    r_pos = lax.broadcasted_iota(jnp.int32, (rows, rows), 1)
    gram_ref[...] = jnp.where(t_pos >= r_pos, gram, 0.0)
    col = col_ref[0, 0]
    row = row_ref[0, 0]
    per_tile = LANES // head_size
    lane = lax.broadcasted_iota(jnp.int32, (half, LANES), 1)
    for c in range(width // LANES):
        lanes = slice(c * LANES, (c + 1) * LANES)
        x_vals = conv_ref[0, 0, :, lanes]
        for part in range(2):
            top = slice(part * half, (part + 1) * half)
            seen = (part + 1) * half
            total = None
            for k in range(per_tile):
                j = c * per_tile + k
                power = col[top, j : j + 1] + row[j : j + 1, :seen]
                decay = jnp.exp2(jnp.minimum(power, 64.0))
                weights = (gram_ref[top, :seen] * decay).astype(BF16)
                y_head = jnp.dot(weights, x_vals[:seen], preferred_element_type=F32)
                total = y_head if k == 0 else jnp.where(lane < k * head_size, total, y_head)
            y_ref[0, 0, top, lanes] = total + skip_ref[0, :, lanes] * x_vals[top].astype(F32)


def outer_kernel(y_ref, c_ref, col_ref, state_ref, z_ref, gain_ref, out_ref, gated_ref, *, head_size):
    rows, width = y_ref.shape[2], y_ref.shape[3]
    c_vals = c_ref[0, 0]
    growth = jnp.exp2(col_ref[0, 0])
    square = jnp.zeros((rows, LANES), F32)
    for c in range(width // LANES):
        lanes = slice(c * LANES, (c + 1) * LANES)
        carried = jnp.dot(c_vals, state_ref[0, c], preferred_element_type=F32)
        spread = lane_pair(growth, c * (LANES // head_size), head_size, rows)
        total = y_ref[0, 0, :, lanes] + spread * carried
        gate = z_ref[0, 0, :, lanes].astype(F32)
        gated = total * (gate * sigmoid(gate))
        gated_ref[:, lanes] = gated
        square = square + gated * gated
    mean_sq = jnp.sum(square, axis=1, keepdims=True) * (1.0 / width)
    factor = jnp.broadcast_to(lax.rsqrt(mean_sq + 1e-05), (rows, LANES))
    for c in range(width // LANES):
        lanes = slice(c * LANES, (c + 1) * LANES)
        out_ref[:, lanes] = (gated_ref[:, lanes] * factor * gain_ref[0, :, lanes]).astype(BF16)


def local(xbc, zgate, dt_raw, a_rate, d_skip, conv_weight, convolution_bias, norm_gain, out_weight):
    seqs, rows, groups, chan = xbc.shape
    heads = a_rate.shape[0]
    per_group = heads // groups
    width = zgate.shape[3]
    head_size = width // per_group
    state_size = (chan - width) // 2
    taps = conv_weight.shape[1]
    cols = out_weight.shape[2]
    if rows != SPAN or state_size % LANES or LANES % head_size:
        raise ValueError("shapes")
    n = lax.axis_size("ctx")
    tp = lax.axis_size("tp")
    chips = n // 2
    nz = 2 ** math.ceil(math.log2(chips) / 2)
    ny = chips // nz
    me = lax.axis_index("ctx")
    core = me % 2
    my_y = (me // 2) % ny
    my_z = me // (2 * ny)

    def send(arr, move):
        pairs = []
        for i in range(n):
            to = move(i // (2 * ny), (i // 2) % ny, i % 2)
            if to is not None:
                pairs.append((i, (to[0] * ny + to[1]) * 2 + to[2]))
        return lax.ppermute(arr, "ctx", pairs)

    def to_core(arr):
        return send(arr, lambda z, y, c: (z, y, 1 - c))

    def to_y(arr, k):
        return send(arr, lambda z, y, c: (z, (y + k) % ny, c))

    def ring_z(arr):
        return send(arr, lambda z, y, c: ((z + 1) % nz, y, c))

    def up_z(arr, k):
        return send(arr, lambda z, y, c: (z + k, y, c) if z + k < nz else None)

    rim = lax.ppermute(xbc[:, rows - (taps - 1) :], "ctx", [(i, i + 1) for i in range(n - 1)])
    rim = jnp.transpose(rim, (0, 2, 1, 3))
    x_in = jnp.transpose(xbc, (0, 2, 1, 3))
    z_in = jnp.transpose(zgate, (0, 2, 1, 3))

    dt = jax.nn.softplus(dt_raw)
    log_decay = dt * (a_rate * (-LOG2E))
    lower = (jnp.arange(rows)[:, None] >= jnp.arange(rows)[None, :]).astype(F32)
    cum = jnp.einsum("tr,srh->sth", lower, log_decay, precision=lax.Precision.HIGHEST)
    last = cum[:, rows - 1]
    scale = jnp.exp2(last[:, None] - cum) * dt

    def by_group(a):
        return jnp.transpose(a.reshape(seqs, rows, groups, per_group), (0, 2, 1, 3))

    cum_col = by_group(cum)
    scale_col = by_group(scale)
    row = jnp.transpose(jnp.log2(dt) - cum, (0, 2, 1)).reshape(seqs, groups, per_group, rows)

    table = jnp.where(jnp.arange(n)[:, None, None] == me, last[None], 0.0)
    table = table + to_core(table)
    part = table
    for _ in range(ny - 1):
        part = to_y(part, 1)
        table = table + part
    part = table
    for _ in range(nz - 1):
        part = ring_z(part)
        table = table + part

    unit_in = out_weight.reshape(groups * width, cols)
    units = {(0, 0, 0): unit_in}
    for dz in range(1, nz):
        units[dz, 0, 0] = ring_z(units[dz - 1, 0, 0])
    for dz in range(nz):
        for dy in range(1, ny):
            units[dz, dy, 0] = to_y(units[dz, dy - 1, 0], 1)
    for dz in range(nz):
        for dy in range(ny):
            units[dz, dy, 1] = to_core(units[dz, dy, 0])

    tiles = width // LANES
    chunk_total = groups * tiles
    grid = (seqs, groups)

    def spec(*block):
        zeros = (0,) * (len(block) - 2)
        return pl.BlockSpec(block, lambda s, g: (s, g) + zeros)

    def group_spec(*block):
        zeros = (0,) * (len(block) - 1)
        return pl.BlockSpec(block, lambda s, g: (g,) + zeros)

    conv_out, state = pl.pallas_call(
        functools.partial(conv_kernel, taps=taps, width=width, head_size=head_size),
        grid=grid,
        in_specs=[
            spec(1, 1, rows, chan),
            spec(1, 1, taps - 1, chan),
            group_spec(1, taps, chan),
            group_spec(1, 1, chan),
            spec(1, 1, rows, per_group),
        ],
        out_specs=[
            spec(1, 1, rows, chan),
            pl.BlockSpec((1, tiles, state_size, LANES), lambda s, g: (s, g, 0, 0)),
        ],
        out_shape=[
            jax.ShapeDtypeStruct((seqs, groups, rows, chan), BF16),
            jax.ShapeDtypeStruct((seqs, chunk_total, state_size, LANES), BF16),
        ],
        scratch_shapes=[pltpu.VMEM((rows + 8, chan), F32)],
        name="conv_state",
        cost_estimate=pl.CostEstimate(flops=2 * 10**9, bytes_accessed=24 * 10**6, transcendentals=10**6),
    )(x_in, rim, conv_weight, convolution_bias[:, None, :], scale_col)

    pieces = 2 * ny
    hp = heads // pieces
    qp = chunk_total // pieces
    logs = table.reshape(nz, ny, 2, seqs, 2, ny, hp)

    def spread(w):
        lead = w.shape[:-1]
        f = jnp.repeat(jnp.exp2(w), head_size, axis=-1)
        return f.reshape(lead + (-1, 1, LANES))

    def pick(a, i, axis):
        return lax.dynamic_index_in_dim(a, i, axis, keepdims=False)

    row_logs = pick(logs, my_z, 0)
    chip_logs = pick(row_logs, my_y, 0)
    halves = state.reshape(seqs, 2, ny, qp, state_size, LANES)
    keep = pick(halves, core, 1)
    away = pick(halves, 1 - core, 1)
    near = to_core(away)
    rest = send(keep, lambda z, y, c: (z, y, 1) if c == 0 else None)
    first = jnp.where(core == 0, keep, near).astype(F32)
    second = jnp.where(core == 0, near, keep).astype(F32)
    chip_half = (spread(pick(chip_logs[1], core, 1)) * first + second).astype(BF16)

    def y_piece(a, k):
        return pick(a, (my_y + k) % ny, 1)

    mine = y_piece(chip_half, 0)
    arrived = {0: mine}
    for k in range(1, ny):
        arrived[k] = to_y(y_piece(chip_half, k), k)
    piece_logs = pick(pick(jnp.sum(logs, axis=2), core, 3), my_y, 3)
    row_piece = pick(piece_logs, my_z, 0)
    tail = jnp.flip(jnp.cumsum(jnp.flip(row_piece, 0), axis=0), 0)
    after = tail - row_piece
    row_total = None
    for k in range(ny):
        src = (my_y - k) % ny
        term = spread(pick(after, src, 0)) * arrived[k].astype(F32)
        row_total = term if row_total is None else row_total + term
    row_send = row_total.astype(BF16)
    z_logs = jnp.sum(piece_logs, axis=1)
    entering = None
    between = jnp.zeros_like(z_logs[0])
    for k in range(1, nz):
        got = up_z(row_send, k).astype(F32)
        term = spread(between) * got
        entering = term if entering is None else entering + term
        between = between + pick(z_logs, (my_z - k) % nz, 0)

    def for_y(k):
        dest = (my_y + k) % ny
        head = jnp.cumsum(row_piece, axis=0) - row_piece
        value = spread(pick(head, dest, 0)) * entering
        for j in range(ny):
            src = (my_y - j) % ny
            weight = spread(pick(tail, (src + 1) % ny, 0) - pick(tail, dest, 0))
            value = value + jnp.where(src < dest, weight * arrived[j].astype(F32), 0.0)
        return value.astype(BF16)

    enter_half = jnp.zeros((seqs, ny, qp, state_size, LANES), BF16)
    for k in range(ny):
        got = for_y(0) if k == 0 else to_y(for_y(k), k)
        enter_half = lax.dynamic_update_index_in_dim(enter_half, got, (my_y - k) % ny, 1)
    other_half = to_core(enter_half)
    low = jnp.where(core == 0, enter_half, other_half)
    high = jnp.where(core == 0, other_half, enter_half)
    chip_enter = jnp.stack([low, high], axis=1).astype(F32)
    core_first = jnp.stack([rest, near], axis=1).astype(F32)
    second_enter = spread(chip_logs[0]) * chip_enter + core_first
    state_in = jnp.where(core == 0, chip_enter, second_enter).astype(BF16)
    state_in = state_in.reshape(seqs, chunk_total, state_size, LANES)

    skip_lanes = jnp.repeat(d_skip.reshape(groups, 1, per_group), head_size, axis=-1)
    y_inner = pl.pallas_call(
        functools.partial(inner_kernel, width=width, head_size=head_size),
        grid=grid,
        in_specs=[
            spec(1, 1, rows, chan),
            spec(1, 1, rows, per_group),
            spec(1, 1, per_group, rows),
            group_spec(1, 1, width),
        ],
        out_specs=spec(1, 1, rows, width),
        out_shape=jax.ShapeDtypeStruct((seqs, groups, rows, width), F32),
        scratch_shapes=[pltpu.VMEM((rows, rows), F32)],
        name="inner",
        cost_estimate=pl.CostEstimate(flops=6 * 10**9, bytes_accessed=14 * 10**6, transcendentals=10**7),
    )(conv_out, cum_col, row, skip_lanes)

    c_block = (width + state_size) // state_size
    normed = pl.pallas_call(
        functools.partial(outer_kernel, head_size=head_size),
        grid=grid,
        in_specs=[
            spec(1, 1, rows, width),
            pl.BlockSpec((1, 1, rows, state_size), lambda s, g: (s, g, 0, c_block)),
            spec(1, 1, rows, per_group),
            pl.BlockSpec((1, tiles, state_size, LANES), lambda s, g: (s, g, 0, 0)),
            spec(1, 1, rows, width),
            group_spec(1, 1, width),
        ],
        out_specs=pl.BlockSpec((rows, width), lambda s, g: (s, g)),
        out_shape=jax.ShapeDtypeStruct((seqs * rows, groups * width), BF16),
        scratch_shapes=[pltpu.VMEM((rows, width), F32)],
        name="outer",
        cost_estimate=pl.CostEstimate(flops=10**9, bytes_accessed=22 * 10**6, transcendentals=3 * 10**6),
    )(y_inner, conv_out, cum_col, state_in, z_in, norm_gain[:, None, :])

    per_tp = n // tp
    me_tp = lax.axis_index("tp")
    out = jnp.zeros((per_tp, seqs * rows, cols), BF16)
    order = sorted(units, key=lambda u: (u[0], u[1], u[2]))
    for dz, dy, dc in order:
        part = jnp.dot(normed, units[dz, dy, dc], preferred_element_type=F32).astype(BF16)

        def source(i):
            z, y, c = i // (2 * ny), (i // 2) % ny, i % 2
            return (((z - dz) % nz) * ny + (y - dy) % ny) * 2 + (c - dc) % 2

        total = part.astype(F32)
        for k in range(1, tp):
            pairs = []
            for i in range(n):
                owner = source(i) // per_tp
                pairs.append((i * tp + (owner + k) % tp, i * tp + owner))
            total = total + lax.ppermute(part, ("ctx", "tp"), pairs).astype(F32)
        src = source(me)
        place = src % per_tp
        held = lax.dynamic_index_in_dim(out, place, 0, keepdims=False)
        value = jnp.where(src // per_tp == me_tp, total.astype(BF16), held)
        out = lax.dynamic_update_index_in_dim(out, value, place, 0)
    out = jnp.transpose(out.reshape(per_tp, seqs, rows, cols), (1, 2, 0, 3))
    return out.reshape(seqs, rows, per_tp * cols)


def solution(mesh):
    placed = (
        P(None, "ctx", "tp", None),
        P(None, "ctx", "tp", None),
        P(None, "ctx", "tp"),
        P("tp"),
        P("tp"),
        P("tp", None, None),
        P("tp", None),
        P("tp", None),
        P("tp", None, "ctx"),
    )
    return jax.shard_map(
        local, mesh=mesh, in_specs=placed, out_specs=P(None, "ctx", "tp"), check_vma=False
    )
```
